256 devices in a mesh: section: 4 (over x), expert: 64 (over y, z, core).
Axes of the slice: x: 4, y: 4, z: 8, core: 2. Of those that a mesh axis runs over, the one named last changes fastest.
Arguments:
- tokens: bfloat16 [6, 1536, 1440], P(None, 'expert'), may hold values from -36 to 36
- norm_gain: float32 [4, 1440], P('section'), may hold values from 0.5 to 1.5
- gate_up: bfloat16 [4, 64, 1440, 2880], P('section', 'expert'), may hold values from -0.15625 to 0.15625
- down: bfloat16 [4, 64, 1440, 1440], P('section', 'expert'), may hold values from -0.15625 to 0.15625
- routes: int32 [4, 6, 1536, 4], P('section', None, 'expert'), may hold values from 0 to 63, all different within a row; in each aligned block of 24 rows (0 to 23, 24 to 47, ..., all dimensions but the last counted through in order) at most 2 rows name the same one
- route_weights: int32 [4, 6, 1536, 4], P('section', None, 'expert'), may hold values from 1 to 4095
Outputs:
- layer_outputs: bfloat16 [4, 6, 1536, 1440], P('section', None, 'expert')
The draws below stay inside these ranges and needn't reach their ends.
Inputs may be any that keep to these rules, and one draw needn't show every extreme that they name: `routes`: each token names 4 different experts; among the 24 tokens of one index of expert in one micro-batch of one layer, no expert is named by more than 2 tokens, a bound that some block reaches.
All inputs are finite; a program needn't handle non-finite values.
Results may differ from the reference program's by a relative error of at most 0.007.
Values may be sent and summed in bfloat16 or wider, within the bound.
No kernel may reach another device: no remote copies, remote signals or barrier semaphores. Data moves between devices by JAX's collectives and lax.ppermute only.
A program may use at most 64 MiB of HBM per device.

```python
import math
import jax
import jax.numpy as jnp
import numpy as np
from jax import lax

D = 1440
HID = 1440
TOP = 4
MICRO = 6
TOK_DEV = 24
LAYERS = 4
EXPERTS = 64
TOKENS = 1536
CAP = 2
N_EXPERT = 64


def draw_tokens(key, part):
    key_rows, key_cols, key_base = jax.random.split(key, 3)
    low = math.log(0.3)
    high = math.log(3.0)
    row_scale = jnp.exp(jax.random.uniform(key_rows, (MICRO, TOKENS, 1), jnp.float32, low, high))
    col_scale = jnp.exp(jax.random.uniform(key_cols, (1, 1, D), jnp.float32, low, high))
    base = jnp.clip(jax.random.normal(key_base, (MICRO, TOKENS, D), jnp.float32), -4.0, 4.0)
    return (base * row_scale * col_scale).astype(jnp.bfloat16)


def place_ends(entries, rng, smallest, largest):
    longest = entries.shape.index(max(entries.shape))
    spots = []
    for shift in (0, 1):
        where = [jax.random.randint(jax.random.fold_in(rng, axis), (), 0, length) for axis, length in enumerate(entries.shape)]
        where[longest] = (where[longest] + shift) % entries.shape[longest]
        spots.append(tuple(where))
    return entries.at[spots[0]].set(smallest).at[spots[1]].set(largest)


def shard_levels(own_key, dims, shards, smallest, high):
    def one(position, parts):
        draws = jax.random.uniform(jax.random.fold_in(jax.random.fold_in(own_key, 6), position), (parts,), jnp.float32, smallest / len(shards), high / len(shards))
        return jnp.repeat(jnp.exp(draws), dims[position] // parts).reshape((-1,) + (1,) * (len(dims) - position - 1))

    gain = one(*shards[0])
    for cut in shards[1:]:
        gain = gain * one(*cut)
    return gain


def shared_out(stream_key, own, number, rows, number_of, top, reach, lean):
    sequence = jax.random.permutation(stream_key, number_of)
    packed, common = load_shares(number_of, rows * top, reach, lean, True), load_shares(number_of, rows * top, reach, lean, False)
    places = jnp.arange(number_of)

    def named(sizes, offset_by):
        used = int((sizes > 0).sum())
        fixed = max(1, used // 4)
        moved = fixed + (places - fixed + offset_by * (used - fixed)) % max(1, number_of - fixed)
        return jnp.zeros((number_of,), jnp.int32).at[sequence[jnp.where(places < fixed, places, moved)]].set(jnp.asarray(sizes, jnp.int32))

    sizes = jnp.where(number % 4 == 0, named(packed, number // 4), named(common, number - number // 4 - 1))
    mixed = jax.random.permutation(jax.random.fold_in(own, 3), number_of)
    giver, receiver = mixed[0:number_of // 2 * 2:2], mixed[1:number_of // 2 * 2:2]
    margin = jnp.minimum(sizes[giver] - 1, reach - sizes[receiver]) // 2
    margin = jnp.where((giver == sequence[0]) | (receiver == sequence[0]) | (sizes[receiver] == 0), 0, jnp.maximum(margin, 0))
    moved = jax.random.randint(jax.random.fold_in(own, 4), (number_of // 2,), 0, 1 << 20) % (margin + 1)
    sizes = sizes.at[giver].add(-moved).at[receiver].add(moved)
    labels = jnp.searchsorted(jnp.cumsum(sizes), jnp.arange(rows * top), side="right").astype(jnp.int32)
    table = labels.reshape(top, rows).T
    table = table[jax.random.permutation(jax.random.fold_in(own, 1), rows)]
    offset_by = jax.random.randint(jax.random.fold_in(own, 2), (rows, 1), 0, top)
    return jnp.take_along_axis(table, (jnp.arange(top)[None, :] + offset_by) % top, axis=1)


def load_shares(count, total, reach, slope, full):
    loads = [(1 << 20) // math.isqrt(rank ** slope) + 1 for rank in range(1, count + 1)]
    largest = reach if full else min(reach, max(-(-total // count), total * loads[0] // sum(loads)))
    least = 1 if total - largest >= count - 1 else 0
    holding, rest = [largest] + [least] * (count - 1), total - largest - least * (count - 1)
    while rest > 0:
        free = [i for i in range(1, count) if holding[i] < largest] or [i for i in range(1, count) if holding[i] < reach]
        pool, budget = sum([loads[i] for i in free]), rest
        for i in free:
            addition = min(reach - holding[i], max(1, budget * loads[i] // pool), rest)
            holding[i] = holding[i] + addition
            rest = rest - addition
    return np.array(holding)


def bell_draw(own_key, dims, spread, limit, cuts=(), kind=jnp.bfloat16):
    drawn = spread * jax.random.normal(own_key, dims, jnp.float32)
    if cuts:
        drawn = drawn * shard_levels(own_key, dims, cuts, -0.22, 0.18)
    return jnp.clip(drawn, -limit, limit).astype(kind)


def setup_inputs(seed: int = 0) -> dict:
    keys = jax.random.split(jax.random.key(seed), 7)
    tokens = draw_tokens(jax.random.fold_in(keys[6], 71), 0)
    norm_gain = jnp.clip(1.0 + 0.1 * jax.random.normal(keys[1], (LAYERS, D), jnp.float32), 0.5, 1.5)
    gate_up = bell_draw(keys[2], (LAYERS, EXPERTS, D, 2 * HID), D ** -0.5, 0.15625, ((0, 4), (1, 64)))
    down = bell_draw(keys[3], (LAYERS, EXPERTS, HID, D), HID ** -0.5, 0.15625, ((0, 4), (1, 64)))
    routes_keys = jax.random.split(jax.random.fold_in(keys[4], 1), LAYERS * MICRO * TOKENS // TOK_DEV)
    routes_turns = jax.random.permutation(jax.random.fold_in(keys[4], 3), LAYERS * MICRO * TOKENS // TOK_DEV)
    routes = jax.vmap(lambda own, number: shared_out(jax.random.fold_in(keys[4], 2), own, number, TOK_DEV, EXPERTS, TOP, CAP, 2))(routes_keys, routes_turns).reshape((LAYERS, MICRO, TOKENS, TOP))
    route_weights = place_ends(jax.random.randint(keys[5], (LAYERS, MICRO, TOKENS, TOP), 1, 4096), jax.random.fold_in(keys[5], 1), 1, 4095).astype(jnp.int32)
    return dict(tokens=tokens, norm_gain=norm_gain, gate_up=gate_up, down=down, routes=routes, route_weights=route_weights)


def expert_rows(normed_rows, flat_routes, gate_up_layer, down_layer):
    row_count = normed_rows.shape[0]
    bound = N_EXPERT * CAP

    def one_expert(outcome, which):
        positions = jnp.nonzero(flat_routes == which, size=bound, fill_value=row_count)[0].astype(jnp.int32)
        picked = jnp.take(normed_rows, jnp.minimum(positions, row_count - 1), axis=0)
        projected = jnp.dot(picked, gate_up_layer[which], preferred_element_type=jnp.float32)
        gate_part = projected[:, :HID]
        up_part = projected[:, HID:]
        activated = (gate_part * jax.nn.sigmoid(1.702 * gate_part) * (up_part + 1.0)).astype(jnp.bfloat16)
        result_rows = jnp.dot(activated, down_layer[which], preferred_element_type=jnp.float32).astype(jnp.bfloat16)
        outcome = outcome.at[positions].set(result_rows.astype(outcome.dtype), mode='drop')
        return (outcome, None)
    start = jnp.zeros((row_count, D), normed_rows.dtype)
    outcome, unused = lax.scan(one_expert, start, jnp.arange(EXPERTS, dtype=jnp.int32))
    return outcome

def reference(tokens, norm_gain, gate_up, down, routes, route_weights):
    current = [tokens[micro_index] for micro_index in range(MICRO)]
    layers_out = []
    for layer in range(LAYERS):
        results = []
        for micro_index in range(MICRO):
            stream = current[micro_index].astype(jnp.float32)
            scale = lax.rsqrt(lax.optimization_barrier(jnp.mean(stream * stream, axis=-1, keepdims=True)) + 1e-05)
            normed = (stream * scale * norm_gain[layer][None, :].astype(jnp.float32)).astype(jnp.bfloat16)
            repeated = jnp.repeat(normed, TOP, axis=0)
            flat_routes = routes[layer, micro_index].reshape(-1)
            expert_out = expert_rows(repeated, flat_routes, gate_up[layer], down[layer]).reshape(TOKENS, TOP, D)
            fixed_point = route_weights[layer, micro_index].astype(jnp.float32)
            shares = fixed_point / lax.optimization_barrier(jnp.sum(fixed_point, axis=-1, keepdims=True))
            mixed = stream + lax.optimization_barrier(jnp.sum(shares[:, :, None] * expert_out.astype(jnp.float32), axis=1))
            results.append(mixed.astype(jnp.bfloat16))
        current = results
        layers_out.append(jnp.stack(results))
    return jnp.stack(layers_out)
```

```python
import jax
import jax.numpy as jnp
from jax import lax
from jax.sharding import PartitionSpec as P

CHUNK = 2


def split_three(value):
    high = lax.reduce_precision(value, 8, 7)
    middle = lax.reduce_precision(value - high, 8, 7)
    low = value - high - middle
    return [part.astype(jnp.bfloat16) for part in (high, middle, low)]


def expert_ffn(rows, gate_up_w, down_w):
    hidden_units = down_w.shape[0]
    projected = jnp.dot(rows, gate_up_w, preferred_element_type=jnp.float32)
    gate_part = projected[:, :hidden_units]
    up_part = projected[:, hidden_units:]
    activated = (gate_part * jax.nn.sigmoid(1.702 * gate_part) * (up_part + 1.0)).astype(
        jnp.bfloat16
    )
    return jnp.dot(activated, down_w, preferred_element_type=jnp.float32).astype(jnp.bfloat16)


def shards(tokens, norm_gain, gate_up, down, routes, route_weights):
    micro_count, token_count, width = tokens.shape
    chosen = routes.shape[-1]
    experts_n = lax.axis_size("expert")
    sections = lax.axis_size("section")
    section_index = lax.axis_index("section")
    chunk_count = micro_count // CHUNK
    rows_n = CHUNK * token_count
    cap = max(2, token_count * chosen * 3 // (2 * experts_n))
    per_expert = CHUNK * cap
    slots = experts_n * per_expert
    gain_row = norm_gain[0]
    gate_up_w = gate_up[0, 0]
    down_w = down[0, 0]

    pairs = routes[0].reshape(micro_count, token_count * chosen)
    order = jnp.arange(token_count * chosen, dtype=jnp.int32)
    same = (pairs[:, :, None] == pairs[:, None, :]) & (order[None, :] < order[:, None])[None]
    rank = jnp.sum(same.astype(jnp.int32), axis=-1)
    block = (jnp.arange(micro_count, dtype=jnp.int32) % CHUNK)[:, None]
    target = (pairs * per_expert + block * cap + rank).reshape(chunk_count, rows_n, chosen)
    fixed_point = route_weights[0].astype(jnp.float32)
    shares = fixed_point / jnp.sum(fixed_point, axis=-1, keepdims=True)
    shares = shares.reshape(chunk_count, rows_n, chosen)
    chunks = tokens.reshape(chunk_count, rows_n, width)

    incoming = jnp.zeros((rows_n, width), jnp.bfloat16)
    results = jnp.zeros((chunk_count, rows_n, width), jnp.bfloat16)
    tick_total = chunk_count + sections - 1
    for tick_number in range(tick_total):
        fresh_input = chunks[min(tick_number, chunk_count - 1)]
        stream = jnp.where(section_index == 0, fresh_input, incoming)
        chunk_here = tick_number - section_index
        clamped = jnp.clip(chunk_here, 0, chunk_count - 1)
        target_rows = lax.dynamic_index_in_dim(target, clamped, 0, keepdims=False)
        share_rows = lax.dynamic_index_in_dim(shares, clamped, 0, keepdims=False)

        slot_ids = jnp.arange(slots, dtype=jnp.int32)
        hits = [slot_ids[:, None] == target_rows[None, :, k] for k in range(chosen)]
        placing = sum(h.astype(jnp.float32) for h in hits).astype(jnp.bfloat16)
        mixing = sum(
            jnp.where(slot_ids[None, :] == target_rows[:, k : k + 1], share_rows[:, k : k + 1], 0.0)
            for k in range(chosen)
        )
        mixing = jnp.concatenate(split_three(mixing), axis=0)

        widened = stream.astype(jnp.float32)
        scale = lax.rsqrt(jnp.mean(widened * widened, axis=-1, keepdims=True) + 1e-05)
        normed = (widened * scale * gain_row[None, :]).astype(jnp.bfloat16)
        outgoing = jnp.dot(placing, normed, preferred_element_type=jnp.float32).astype(jnp.bfloat16)
        outgoing = outgoing.reshape(experts_n, per_expert, width)
        arrived = lax.all_to_all(outgoing, "expert", split_axis=0, concat_axis=0, tiled=True)
        computed = expert_ffn(arrived.reshape(slots, width), gate_up_w, down_w)
        computed = computed.reshape(experts_n, per_expert, width)
        returned = lax.all_to_all(computed, "expert", split_axis=0, concat_axis=0, tiled=True)
        returned_rows = returned.reshape(slots, width)
        mixed = jnp.dot(mixing, returned_rows, preferred_element_type=jnp.float32)
        mixed = mixed.reshape(3, rows_n, width)
        output_rows = (widened + (mixed[0] + (mixed[1] + mixed[2]))).astype(jnp.bfloat16)

        active = jnp.logical_and(chunk_here >= 0, chunk_here < chunk_count)
        kept = lax.dynamic_index_in_dim(results, clamped, 0, keepdims=False)
        results = lax.dynamic_update_index_in_dim(
            results, jnp.where(active, output_rows, kept), clamped, 0
        )
        if tick_number + 1 < tick_total:
            incoming = lax.ppermute(
                output_rows, "section", [(s, s + 1) for s in range(sections - 1)]
            )
    return results.reshape(1, micro_count, token_count, width)


def solution(mesh):
    return jax.shard_map(
        shards,
        mesh=mesh,
        in_specs=(
            P(None, "expert", None),
            P("section", None),
            P("section", "expert", None, None),
            P("section", "expert", None, None),
            P("section", None, "expert", None),
            P("section", None, "expert", None),
        ),
        out_specs=P("section", None, "expert", None),
        check_vma=False,
    )
```

```python
import jax
import jax.numpy as jnp
from jax import lax
from jax.experimental import pallas as pl
from jax.experimental.pallas import tpu as pltpu
from jax.sharding import PartitionSpec as P

CHUNK = 2
ROW_STEP = 32
COLUMN_BLOCKS = ((0, 1024), (1024, 1920), (1920, 2880))


def split_three(value):
    high = lax.reduce_precision(value, 8, 7)
    middle = lax.reduce_precision(value - high, 8, 7)
    low = value - high - middle
    return [part.astype(jnp.bfloat16) for part in (high, middle, low)]


def ffn_kernel(x_ref, gate_up_ref, down_ref, out_ref, gate_up_here, down_here, projected, activated, sems):
    experts_n, per_expert, width = x_ref.shape
    slots = experts_n * per_expert
    hidden_units = down_ref.shape[0]
    arriving = []
    for number, (first, last) in enumerate(COLUMN_BLOCKS):
        part = pl.ds(first, last - first)
        arriving.append(
            pltpu.make_async_copy(
                gate_up_ref.at[:, part], gate_up_here.at[:, part], sems.at[number]
            )
        )
    down_copy = pltpu.make_async_copy(down_ref, down_here, sems.at[len(COLUMN_BLOCKS)])
    for copy in arriving:
        copy.start()
    rows = x_ref[...].reshape(slots, width)
    for number, (first, last) in enumerate(COLUMN_BLOCKS):
        arriving[number].wait()
        if number == 0:
            down_copy.start()
        projected[:, first:last] = jnp.dot(
            rows, gate_up_here[:, first:last], preferred_element_type=jnp.float32
        )
    for first in range(0, slots, ROW_STEP):
        part = slice(first, first + ROW_STEP)
        gate_part = projected[part, :hidden_units]
        up_part = projected[part, hidden_units:]
        activated[part, :] = (
            gate_part * jax.nn.sigmoid(1.702 * gate_part) * (up_part + 1.0)
        ).astype(jnp.bfloat16)
    down_copy.wait()
    result = jnp.dot(activated[...], down_here[...], preferred_element_type=jnp.float32)
    out_ref[...] = result.reshape(experts_n, per_expert, width).astype(jnp.bfloat16)


def expert_ffn(arrived, gate_up_w, down_w):
    experts_n, per_expert, width = arrived.shape
    slots = experts_n * per_expert
    hidden_units = down_w.shape[0]
    whole = pl.BlockSpec(memory_space=pltpu.VMEM)
    outside = pl.BlockSpec(memory_space=pltpu.HBM)
    return pl.pallas_call(
        ffn_kernel,
        out_shape=jax.ShapeDtypeStruct(arrived.shape, arrived.dtype),
        in_specs=[whole, outside, outside],
        out_specs=whole,
        scratch_shapes=[
            pltpu.VMEM(gate_up_w.shape, gate_up_w.dtype),
            pltpu.VMEM(down_w.shape, down_w.dtype),
            pltpu.VMEM((slots, 2 * hidden_units), jnp.float32),
            pltpu.VMEM((slots, hidden_units), jnp.bfloat16),
            pltpu.SemaphoreType.DMA((len(COLUMN_BLOCKS) + 1,)),
        ],
        compiler_params=pltpu.CompilerParams(vmem_limit_bytes=40 << 20),
    )(
        arrived,
        pltpu.with_memory_space_constraint(gate_up_w, pltpu.HBM),
        pltpu.with_memory_space_constraint(down_w, pltpu.HBM),
    )


def shards(tokens, norm_gain, gate_up, down, routes, route_weights):
    micro_count, token_count, width = tokens.shape
    chosen = routes.shape[-1]
    experts_n = lax.axis_size("expert")
    sections = lax.axis_size("section")
    section_index = lax.axis_index("section")
    chunk_count = micro_count // CHUNK
    rows_n = CHUNK * token_count
    cap = max(2, token_count * chosen * 3 // (2 * experts_n))
    per_expert = CHUNK * cap
    slots = experts_n * per_expert
    gain_row = norm_gain[0]
    gate_up_w = gate_up[0, 0]
    down_w = down[0, 0]

    pairs = routes[0].reshape(micro_count, token_count * chosen)
    order = jnp.arange(token_count * chosen, dtype=jnp.int32)
    same = (pairs[:, :, None] == pairs[:, None, :]) & (order[None, :] < order[:, None])[None]
    rank = jnp.sum(same.astype(jnp.int32), axis=-1)
    block = (jnp.arange(micro_count, dtype=jnp.int32) % CHUNK)[:, None]
    target = (pairs * per_expert + block * cap + rank).reshape(chunk_count, rows_n, chosen)
    fixed_point = route_weights[0].astype(jnp.float32)
    shares = fixed_point / jnp.sum(fixed_point, axis=-1, keepdims=True)
    shares = shares.reshape(chunk_count, rows_n, chosen)
    chunks = tokens.reshape(chunk_count, rows_n, width)

    slot_ids = jnp.arange(slots, dtype=jnp.int32)

    def step(tick_number, stream, results):
        chunk_here = tick_number - section_index
        clamped = jnp.clip(chunk_here, 0, chunk_count - 1)
        target_rows = lax.dynamic_index_in_dim(target, clamped, 0, keepdims=False)
        share_rows = lax.dynamic_index_in_dim(shares, clamped, 0, keepdims=False)
        hits = [slot_ids[:, None] == target_rows[None, :, k] for k in range(chosen)]
        placing = sum(h.astype(jnp.float32) for h in hits).astype(jnp.bfloat16)
        mixing = sum(
            jnp.where(slot_ids[None, :] == target_rows[:, k : k + 1], share_rows[:, k : k + 1], 0.0)
            for k in range(chosen)
        )
        mixing = jnp.concatenate(split_three(mixing), axis=0)

        widened = stream.astype(jnp.float32)
        scale = lax.rsqrt(jnp.mean(widened * widened, axis=-1, keepdims=True) + 1e-05)
        normed = (widened * scale * gain_row[None, :]).astype(jnp.bfloat16)
        outgoing = jnp.dot(placing, normed, preferred_element_type=jnp.float32).astype(jnp.bfloat16)
        outgoing = outgoing.reshape(experts_n, per_expert, width)
        arrived = lax.all_to_all(outgoing, "expert", split_axis=0, concat_axis=0, tiled=True)
        computed = expert_ffn(arrived, gate_up_w, down_w)
        returned = lax.all_to_all(computed, "expert", split_axis=0, concat_axis=0, tiled=True)
        returned_rows = returned.reshape(slots, width)
        mixed = jnp.dot(mixing, returned_rows, preferred_element_type=jnp.float32)
        mixed = mixed.reshape(3, rows_n, width)
        output_rows = (widened + (mixed[0] + (mixed[1] + mixed[2]))).astype(jnp.bfloat16)

        active = jnp.logical_and(chunk_here >= 0, chunk_here < chunk_count)
        kept = lax.dynamic_index_in_dim(results, clamped, 0, keepdims=False)
        results = lax.dynamic_update_index_in_dim(
            results, jnp.where(active, output_rows, kept), clamped, 0
        )
        return output_rows, results

    def relayed(tick_number, carried):
        previous, results = carried
        incoming = lax.ppermute(previous, "section", [(s, (s + 1) % sections) for s in range(sections)])
        fresh_input = lax.dynamic_index_in_dim(
            chunks, jnp.minimum(tick_number, chunk_count - 1), 0, keepdims=False
        )
        return step(tick_number, jnp.where(section_index == 0, fresh_input, incoming), results)

    results = jnp.zeros((chunk_count, rows_n, width), jnp.bfloat16)
    first_stream = jnp.where(section_index == 0, chunks[0], jnp.zeros_like(chunks[0]))
    carried = step(0, first_stream, results)
    carried = lax.fori_loop(1, chunk_count + sections - 1, relayed, carried)
    return carried[1].reshape(1, micro_count, token_count, width)


def solution(mesh):
    return jax.shard_map(
        shards,
        mesh=mesh,
        in_specs=(
            P(None, "expert", None),
            P("section", None),
            P("section", "expert", None, None),
            P("section", "expert", None, None),
            P("section", None, "expert", None),
            P("section", None, "expert", None),
        ),
        out_specs=P("section", None, "expert", None),
        check_vma=False,
    )
```

```python
import jax
import jax.numpy as jnp
from jax import lax
from jax.experimental import pallas as pl
from jax.experimental.pallas import tpu as pltpu
from jax.sharding import PartitionSpec as P

CHUNK = 2
ROW_STEP = 32
COLUMN_BLOCKS = ((0, 1024), (1024, 1920), (1920, 2880))


def split_three(value):
    high = lax.reduce_precision(value, 8, 7)
    middle = lax.reduce_precision(value - high, 8, 7)
    low = value - high - middle
    return [part.astype(jnp.bfloat16) for part in (high, middle, low)]


def ffn_kernel(x_ref, gate_up_ref, down_ref, out_ref, gate_up_here, down_here, projected, activated, sems):
    experts_n, per_expert, width = x_ref.shape
    slots = experts_n * per_expert
    hidden_units = down_ref.shape[0]
    arriving = []
    for number, (first, last) in enumerate(COLUMN_BLOCKS):
        part = pl.ds(first, last - first)
        arriving.append(
            pltpu.make_async_copy(
                gate_up_ref.at[:, part], gate_up_here.at[:, part], sems.at[number]
            )
        )
    down_copy = pltpu.make_async_copy(down_ref, down_here, sems.at[len(COLUMN_BLOCKS)])
    for copy in arriving:
        copy.start()
    rows = x_ref[...].reshape(slots, width)
    for number, (first, last) in enumerate(COLUMN_BLOCKS):
        arriving[number].wait()
        if number == 0:
            down_copy.start()
        projected[:, first:last] = jnp.dot(
            rows, gate_up_here[:, first:last], preferred_element_type=jnp.float32
        )
    for first in range(0, slots, ROW_STEP):
        part = slice(first, first + ROW_STEP)
        gate_part = projected[part, :hidden_units]
        up_part = projected[part, hidden_units:]
        activated[part, :] = (
            gate_part * jax.nn.sigmoid(1.702 * gate_part) * (up_part + 1.0)
        ).astype(jnp.bfloat16)
    down_copy.wait()
    result = jnp.dot(activated[...], down_here[...], preferred_element_type=jnp.float32)
    out_ref[...] = result.reshape(experts_n, per_expert, width).astype(jnp.bfloat16)


def expert_ffn(arrived, gate_up_w, down_w):
    experts_n, per_expert, width = arrived.shape
    slots = experts_n * per_expert
    hidden_units = down_w.shape[0]
    whole = pl.BlockSpec(memory_space=pltpu.VMEM)
    outside = pl.BlockSpec(memory_space=pltpu.HBM)
    return pl.pallas_call(
        ffn_kernel,
        out_shape=jax.ShapeDtypeStruct(arrived.shape, arrived.dtype),
        in_specs=[whole, outside, outside],
        out_specs=whole,
        scratch_shapes=[
            pltpu.VMEM(gate_up_w.shape, gate_up_w.dtype),
            pltpu.VMEM(down_w.shape, down_w.dtype),
            pltpu.VMEM((slots, 2 * hidden_units), jnp.float32),
            pltpu.VMEM((slots, hidden_units), jnp.bfloat16),
            pltpu.SemaphoreType.DMA((len(COLUMN_BLOCKS) + 1,)),
        ],
        compiler_params=pltpu.CompilerParams(vmem_limit_bytes=40 << 20),
    )(
        arrived,
        pltpu.with_memory_space_constraint(gate_up_w, pltpu.HBM),
        pltpu.with_memory_space_constraint(down_w, pltpu.HBM),
    )


def shards(tokens, norm_gain, gate_up, down, routes, route_weights):
    micro_count, token_count, width = tokens.shape
    chosen = routes.shape[-1]
    experts_n = lax.axis_size("expert")
    sections = lax.axis_size("section")
    section_index = lax.axis_index("section")
    chunk_count = micro_count // CHUNK
    rows_n = CHUNK * token_count
    cap = max(2, token_count * chosen * 3 // (2 * experts_n))
    per_expert = CHUNK * cap
    slots = experts_n * per_expert
    gain_row = norm_gain[0]
    gate_up_w = gate_up[0, 0]
    down_w = down[0, 0]

    pairs = routes[0].reshape(micro_count, token_count * chosen)
    order = jnp.arange(token_count * chosen, dtype=jnp.int32)
    same = (pairs[:, :, None] == pairs[:, None, :]) & (order[None, :] < order[:, None])[None]
    rank = jnp.sum(same.astype(jnp.int32), axis=-1)
    block = (jnp.arange(micro_count, dtype=jnp.int32) % CHUNK)[:, None]
    target = (pairs * per_expert + block * cap + rank).reshape(chunk_count, rows_n, chosen)
    fixed_point = route_weights[0].astype(jnp.float32)
    shares = fixed_point / jnp.sum(fixed_point, axis=-1, keepdims=True)
    shares = shares.reshape(chunk_count, rows_n, chosen)
    chunks = tokens.reshape(chunk_count, rows_n, width)

    slot_ids = jnp.arange(slots, dtype=jnp.int32)

    def step(tick_number, stream, results, ahead):
        chunk_here = tick_number - section_index
        clamped = jnp.clip(chunk_here, 0, chunk_count - 1)
        target_rows = lax.dynamic_index_in_dim(target, clamped, 0, keepdims=False)
        share_rows = lax.dynamic_index_in_dim(shares, clamped, 0, keepdims=False)
        hits = [slot_ids[:, None] == target_rows[None, :, k] for k in range(chosen)]
        placing = sum(h.astype(jnp.float32) for h in hits).astype(jnp.bfloat16)
        mixing = sum(
            jnp.where(slot_ids[None, :] == target_rows[:, k : k + 1], share_rows[:, k : k + 1], 0.0)
            for k in range(chosen)
        )
        mixing = jnp.concatenate(split_three(mixing), axis=0)

        widened = stream.astype(jnp.float32)
        scale = lax.rsqrt(jnp.mean(widened * widened, axis=-1, keepdims=True) + 1e-05)
        normed = (widened * scale * gain_row[None, :]).astype(jnp.bfloat16)
        outgoing = jnp.dot(placing, normed, preferred_element_type=jnp.float32).astype(jnp.bfloat16)
        outgoing = outgoing.reshape(experts_n, per_expert, width)
        active = jnp.logical_and(chunk_here >= 0, chunk_here < chunk_count)
        kept = lax.dynamic_index_in_dim(results, clamped, 0, keepdims=False)
        place = clamped.astype(jnp.uint32)
        if ahead:
            outgoing, mixing, kept, active, place = lax.optimization_barrier(
                (outgoing, mixing, kept, active, place)
            )
        arrived = lax.all_to_all(outgoing, "expert", split_axis=0, concat_axis=0, tiled=True)
        computed = expert_ffn(arrived, gate_up_w, down_w)
        returned = lax.all_to_all(computed, "expert", split_axis=0, concat_axis=0, tiled=True)
        returned_rows = returned.reshape(slots, width)
        mixed = jnp.dot(mixing, returned_rows, preferred_element_type=jnp.float32)
        mixed = mixed.reshape(3, rows_n, width)
        output_rows = (widened + (mixed[0] + (mixed[1] + mixed[2]))).astype(jnp.bfloat16)

        results = lax.dynamic_update_slice(
            results,
            jnp.where(active, output_rows, kept)[None],
            (place, jnp.uint32(0), jnp.uint32(0)),
        )
        return output_rows, results

    def relayed(tick_number, carried):
        previous, results = carried
        incoming = lax.ppermute(previous, "section", [(s, (s + 1) % sections) for s in range(sections)])
        fresh_input = lax.dynamic_index_in_dim(
            chunks, jnp.minimum(tick_number, chunk_count - 1), 0, keepdims=False
        )
        return step(tick_number, jnp.where(section_index == 0, fresh_input, incoming), results, True)

    results = jnp.zeros((chunk_count, rows_n, width), jnp.bfloat16)
    first_stream = jnp.where(section_index == 0, chunks[0], jnp.zeros_like(chunks[0]))
    carried = step(0, first_stream, results, False)
    carried = lax.fori_loop(1, chunk_count + sections - 1, relayed, carried)
    return carried[1].reshape(1, micro_count, token_count, width)


def solution(mesh):
    return jax.shard_map(
        shards,
        mesh=mesh,
        in_specs=(
            P(None, "expert", None),
            P("section", None),
            P("section", "expert", None, None),
            P("section", "expert", None, None),
            P("section", None, "expert", None),
            P("section", None, "expert", None),
        ),
        out_specs=P("section", None, "expert", None),
        check_vma=False,
    )
```

```python
import jax
import jax.numpy as jnp
from jax import lax
from jax.experimental import pallas as pl
from jax.experimental.pallas import tpu as pltpu
from jax.sharding import PartitionSpec as P

CHUNK = 2
CAP = 2
ROW_STEP = 32
COLUMN_BLOCKS = ((0, 1024), (1024, 1920), (1920, 2880))


def split_three(value):
    high = lax.reduce_precision(value, 8, 7)
    middle = lax.reduce_precision(value - high, 8, 7)
    low = value - high - middle
    return [part.astype(jnp.bfloat16) for part in (high, middle, low)]


def ffn_kernel(x_ref, gate_up_ref, down_ref, out_ref, gate_up_here, down_here, projected, activated, sems):
    experts_n, per_expert, width = x_ref.shape
    slots = experts_n * per_expert
    hidden_units = down_ref.shape[0]
    arriving = []
    for number, (first, last) in enumerate(COLUMN_BLOCKS):
        part = pl.ds(first, last - first)
        arriving.append(
            pltpu.make_async_copy(
                gate_up_ref.at[:, part], gate_up_here.at[:, part], sems.at[number]
            )
        )
    down_copy = pltpu.make_async_copy(down_ref, down_here, sems.at[len(COLUMN_BLOCKS)])
    for copy in arriving:
        copy.start()
    rows = x_ref[...].reshape(slots, width)
    for number, (first, last) in enumerate(COLUMN_BLOCKS):
        arriving[number].wait()
        if number == 0:
            down_copy.start()
        projected[:, first:last] = jnp.dot(
            rows, gate_up_here[:, first:last], preferred_element_type=jnp.float32
        )
    for first in range(0, slots, ROW_STEP):
        part = slice(first, first + ROW_STEP)
        gate_part = projected[part, :hidden_units]
        up_part = projected[part, hidden_units:]
        activated[part, :] = (
            gate_part * jax.nn.sigmoid(1.702 * gate_part) * (up_part + 1.0)
        ).astype(jnp.bfloat16)
    down_copy.wait()
    result = jnp.dot(activated[...], down_here[...], preferred_element_type=jnp.float32)
    out_ref[...] = result.reshape(experts_n, per_expert, width).astype(jnp.bfloat16)


def place_kernel(section_ref, incoming_ref, fresh_ref, gain_ref, target_ref, out_ref, stream_ref):
    experts_n, per_expert, width = out_ref.shape
    slots = experts_n * per_expert
    rows_n = incoming_ref.shape[0]
    stream = jnp.where(
        section_ref[0] == 0, fresh_ref[...].astype(jnp.float32), incoming_ref[...].astype(jnp.float32)
    )
    stream_ref[...] = stream.astype(jnp.bfloat16)
    scale = lax.rsqrt(jnp.mean(stream * stream, axis=-1, keepdims=True) + 1e-05)
    normed = (stream * scale * gain_ref[...]).astype(jnp.bfloat16)
    slot_ids = lax.broadcasted_iota(jnp.int32, (slots, rows_n), 0)
    placing = jnp.zeros((slots, rows_n), jnp.float32)
    for choice in range(target_ref.shape[0]):
        placing += jnp.where(slot_ids == target_ref[choice : choice + 1, :], 1.0, 0.0)
    outgoing = jnp.dot(placing.astype(jnp.bfloat16), normed, preferred_element_type=jnp.float32)
    out_ref[...] = outgoing.reshape(experts_n, per_expert, width).astype(jnp.bfloat16)


def place(section, incoming, fresh, gain, target_columns, experts_n):
    rows_n, width = incoming.shape
    per_expert = CHUNK * CAP
    whole = pl.BlockSpec(memory_space=pltpu.VMEM)
    return pl.pallas_call(
        place_kernel,
        out_shape=(
            jax.ShapeDtypeStruct((experts_n, per_expert, width), jnp.bfloat16),
            jax.ShapeDtypeStruct((rows_n, width), jnp.bfloat16),
        ),
        in_specs=[pl.BlockSpec(memory_space=pltpu.SMEM)] + [whole] * 4,
        out_specs=(whole, whole),
        compiler_params=pltpu.CompilerParams(vmem_limit_bytes=16 << 20),
    )(section, incoming, fresh, gain, target_columns)


def combine_kernel(returned_ref, mixing_ref, stream_ref, out_ref):
    experts_n, per_expert, width = returned_ref.shape
    rows_n = stream_ref.shape[0]
    rows = returned_ref[...].reshape(experts_n * per_expert, width)
    mixed = jnp.dot(mixing_ref[...], rows, preferred_element_type=jnp.float32)
    total = mixed[:rows_n] + (mixed[rows_n : 2 * rows_n] + mixed[2 * rows_n :])
    out_ref[...] = (stream_ref[...].astype(jnp.float32) + total).astype(jnp.bfloat16)


def combine(returned, mixing, stream):
    whole = pl.BlockSpec(memory_space=pltpu.VMEM)
    return pl.pallas_call(
        combine_kernel,
        out_shape=jax.ShapeDtypeStruct(stream.shape, stream.dtype),
        in_specs=[whole] * 3,
        out_specs=whole,
        compiler_params=pltpu.CompilerParams(vmem_limit_bytes=16 << 20),
    )(returned, mixing, stream)


def expert_ffn(arrived, gate_up_w, down_w):
    experts_n, per_expert, width = arrived.shape
    slots = experts_n * per_expert
    hidden_units = down_w.shape[0]
    whole = pl.BlockSpec(memory_space=pltpu.VMEM)
    outside = pl.BlockSpec(memory_space=pltpu.HBM)
    return pl.pallas_call(
        ffn_kernel,
        out_shape=jax.ShapeDtypeStruct(arrived.shape, arrived.dtype),
        in_specs=[whole, outside, outside],
        out_specs=whole,
        scratch_shapes=[
            pltpu.VMEM(gate_up_w.shape, gate_up_w.dtype),
            pltpu.VMEM(down_w.shape, down_w.dtype),
            pltpu.VMEM((slots, 2 * hidden_units), jnp.float32),
            pltpu.VMEM((slots, hidden_units), jnp.bfloat16),
            pltpu.SemaphoreType.DMA((len(COLUMN_BLOCKS) + 1,)),
        ],
        compiler_params=pltpu.CompilerParams(vmem_limit_bytes=40 << 20),
    )(
        arrived,
        pltpu.with_memory_space_constraint(gate_up_w, pltpu.HBM),
        pltpu.with_memory_space_constraint(down_w, pltpu.HBM),
    )


def shards(tokens, norm_gain, gate_up, down, routes, route_weights):
    micro_count, token_count, width = tokens.shape
    chosen = routes.shape[-1]
    experts_n = lax.axis_size("expert")
    sections = lax.axis_size("section")
    section_index = lax.axis_index("section")
    chunk_count = micro_count // CHUNK
    rows_n = CHUNK * token_count
    per_expert = CHUNK * CAP
    slots = experts_n * per_expert
    gate_up_w = gate_up[0, 0]
    down_w = down[0, 0]

    pairs = routes[0].reshape(micro_count, token_count * chosen)
    order = jnp.arange(token_count * chosen, dtype=jnp.int32)
    same = (pairs[:, :, None] == pairs[:, None, :]) & (order[None, :] < order[:, None])[None]
    rank = jnp.sum(same.astype(jnp.int32), axis=-1)
    block = (jnp.arange(micro_count, dtype=jnp.int32) % CHUNK)[:, None]
    target = (pairs * per_expert + block * CAP + rank).reshape(chunk_count, rows_n, chosen)
    fixed_point = route_weights[0].astype(jnp.float32)
    shares = fixed_point / jnp.sum(fixed_point, axis=-1, keepdims=True)
    shares = shares.reshape(chunk_count, rows_n, chosen)
    chunks = tokens.reshape(chunk_count, rows_n, width)

    slot_ids = jnp.arange(slots, dtype=jnp.int32)

    section_scalar = section_index.reshape(1).astype(jnp.int32)

    def step(tick_number, incoming, fresh_input, results, ahead):
        chunk_here = tick_number - section_index
        clamped = jnp.clip(chunk_here, 0, chunk_count - 1)
        target_rows = lax.dynamic_index_in_dim(target, clamped, 0, keepdims=False)
        share_rows = lax.dynamic_index_in_dim(shares, clamped, 0, keepdims=False)
        mixing = sum(
            jnp.where(slot_ids[None, :] == target_rows[:, k : k + 1], share_rows[:, k : k + 1], 0.0)
            for k in range(chosen)
        )
        mixing = jnp.concatenate(split_three(mixing), axis=0)
        outgoing, stream = place(
            section_scalar, incoming, fresh_input, norm_gain, target_rows.T, experts_n
        )
        active = jnp.logical_and(chunk_here >= 0, chunk_here < chunk_count)
        kept = lax.dynamic_index_in_dim(results, clamped, 0, keepdims=False)
        place_at = clamped.astype(jnp.uint32)
        if ahead:
            outgoing, mixing, kept, active, place_at = lax.optimization_barrier(
                (outgoing, mixing, kept, active, place_at)
            )
        arrived = lax.all_to_all(outgoing, "expert", split_axis=0, concat_axis=0, tiled=True)
        computed = expert_ffn(arrived, gate_up_w, down_w)
        returned = lax.all_to_all(computed, "expert", split_axis=0, concat_axis=0, tiled=True)
        output_rows = combine(returned, mixing, stream)
        results = lax.dynamic_update_slice(
            results,
            jnp.where(active, output_rows, kept)[None],
            (place_at, jnp.uint32(0), jnp.uint32(0)),
        )
        return output_rows, results

    def relayed(tick_number, carried):
        previous, results = carried
        incoming = lax.ppermute(
            previous, "section", [(s, (s + 1) % sections) for s in range(sections)]
        )
        fresh_input = lax.dynamic_index_in_dim(
            chunks, jnp.minimum(tick_number, chunk_count - 1), 0, keepdims=False
        )
        return step(tick_number, incoming, fresh_input, results, True)

    results = jnp.zeros((chunk_count, rows_n, width), jnp.bfloat16)
    carried = step(0, jnp.zeros_like(chunks[0]), chunks[0], results, False)
    carried = lax.fori_loop(1, chunk_count + sections - 1, relayed, carried)
    return carried[1].reshape(1, micro_count, token_count, width)


def solution(mesh):
    return jax.shard_map(
        shards,
        mesh=mesh,
        in_specs=(
            P(None, "expert", None),
            P("section", None),
            P("section", "expert", None, None),
            P("section", "expert", None, None),
            P("section", None, "expert", None),
            P("section", None, "expert", None),
        ),
        out_specs=P("section", None, "expert", None),
        check_vma=False,
    )
```

```python
import jax
import jax.numpy as jnp
from jax import lax
from jax.experimental import pallas as pl
from jax.experimental.pallas import tpu as pltpu
from jax.sharding import PartitionSpec as P

CHUNK = 2
CAP = 2
ROW_STEP = 32
COLUMN_BLOCKS = ((0, 1024), (1024, 1920), (1920, 2880))


def split_three(value):
    high = lax.reduce_precision(value, 8, 7)
    middle = lax.reduce_precision(value - high, 8, 7)
    low = value - high - middle
    return [part.astype(jnp.bfloat16) for part in (high, middle, low)]


def ffn_kernel(x_ref, gate_up_ref, down_ref, out_ref, gate_up_here, down_here, projected, activated, sems):
    experts_n, per_expert, width = x_ref.shape
    slots = experts_n * per_expert
    hidden_units = down_ref.shape[0]
    arriving = []
    for number, (first, last) in enumerate(COLUMN_BLOCKS):
        part = pl.ds(first, last - first)
        arriving.append(
            pltpu.make_async_copy(
                gate_up_ref.at[:, part], gate_up_here.at[:, part], sems.at[number]
            )
        )
    down_copy = pltpu.make_async_copy(down_ref, down_here, sems.at[len(COLUMN_BLOCKS)])
    for copy in arriving:
        copy.start()
    rows = x_ref[...].reshape(slots, width)
    for number, (first, last) in enumerate(COLUMN_BLOCKS):
        arriving[number].wait()
        if number == 0:
            down_copy.start()
        projected[:, first:last] = jnp.dot(
            rows, gate_up_here[:, first:last], preferred_element_type=jnp.float32
        )
    for first in range(0, slots, ROW_STEP):
        part = slice(first, first + ROW_STEP)
        gate_part = projected[part, :hidden_units]
        up_part = projected[part, hidden_units:]
        activated[part, :] = (
            gate_part * jax.nn.sigmoid(1.702 * gate_part) * (up_part + 1.0)
        ).astype(jnp.bfloat16)
    down_copy.wait()
    result = jnp.dot(activated[...], down_here[...], preferred_element_type=jnp.float32)
    out_ref[...] = result.reshape(experts_n, per_expert, width).astype(jnp.bfloat16)


def place_kernel(section_ref, incoming_ref, fresh_ref, gain_ref, target_ref, out_ref, stream_ref):
    experts_n, per_expert, width = out_ref.shape
    slots = experts_n * per_expert
    rows_n = incoming_ref.shape[0]
    stream = jnp.where(
        section_ref[0] == 0, fresh_ref[...].astype(jnp.float32), incoming_ref[...].astype(jnp.float32)
    )
    stream_ref[...] = stream.astype(jnp.bfloat16)
    scale = lax.rsqrt(jnp.mean(stream * stream, axis=-1, keepdims=True) + 1e-05)
    normed = (stream * scale * gain_ref[...]).astype(jnp.bfloat16)
    slot_ids = lax.broadcasted_iota(jnp.int32, (slots, rows_n), 0)
    placing = jnp.zeros((slots, rows_n), jnp.float32)
    for choice in range(target_ref.shape[0]):
        placing += jnp.where(slot_ids == target_ref[choice : choice + 1, :], 1.0, 0.0)
    outgoing = jnp.dot(placing.astype(jnp.bfloat16), normed, preferred_element_type=jnp.float32)
    out_ref[...] = outgoing.reshape(experts_n, per_expert, width).astype(jnp.bfloat16)


def place(section, incoming, fresh, gain, target_columns, experts_n):
    rows_n, width = incoming.shape
    per_expert = CHUNK * CAP
    whole = pl.BlockSpec(memory_space=pltpu.VMEM)
    return pl.pallas_call(
        place_kernel,
        out_shape=(
            jax.ShapeDtypeStruct((experts_n, per_expert, width), jnp.bfloat16),
            jax.ShapeDtypeStruct((rows_n, width), jnp.bfloat16),
        ),
        in_specs=[pl.BlockSpec(memory_space=pltpu.SMEM)] + [whole] * 4,
        out_specs=(whole, whole),
        compiler_params=pltpu.CompilerParams(vmem_limit_bytes=16 << 20),
    )(section, incoming, fresh, gain, target_columns)


def combine_kernel(returned_ref, mixing_ref, stream_ref, out_ref):
    experts_n, per_expert, width = returned_ref.shape
    rows_n = stream_ref.shape[0]
    rows = returned_ref[...].reshape(experts_n * per_expert, width)
    mixed = jnp.dot(mixing_ref[...], rows, preferred_element_type=jnp.float32)
    total = mixed[:rows_n] + (mixed[rows_n : 2 * rows_n] + mixed[2 * rows_n :])
    out_ref[...] = (stream_ref[...].astype(jnp.float32) + total).astype(jnp.bfloat16)


def combine(returned, mixing, stream):
    whole = pl.BlockSpec(memory_space=pltpu.VMEM)
    return pl.pallas_call(
        combine_kernel,
        out_shape=jax.ShapeDtypeStruct(stream.shape, stream.dtype),
        in_specs=[whole] * 3,
        out_specs=whole,
        compiler_params=pltpu.CompilerParams(vmem_limit_bytes=16 << 20),
    )(returned, mixing, stream)


def expert_ffn(arrived, gate_up_w, down_w):
    experts_n, per_expert, width = arrived.shape
    slots = experts_n * per_expert
    hidden_units = down_w.shape[0]
    whole = pl.BlockSpec(memory_space=pltpu.VMEM)
    outside = pl.BlockSpec(memory_space=pltpu.HBM)
    return pl.pallas_call(
        ffn_kernel,
        out_shape=jax.ShapeDtypeStruct(arrived.shape, arrived.dtype),
        in_specs=[whole, outside, outside],
        out_specs=whole,
        scratch_shapes=[
            pltpu.VMEM(gate_up_w.shape, gate_up_w.dtype),
            pltpu.VMEM(down_w.shape, down_w.dtype),
            pltpu.VMEM((slots, 2 * hidden_units), jnp.float32),
            pltpu.VMEM((slots, hidden_units), jnp.bfloat16),
            pltpu.SemaphoreType.DMA((len(COLUMN_BLOCKS) + 1,)),
        ],
        compiler_params=pltpu.CompilerParams(vmem_limit_bytes=40 << 20),
    )(
        arrived,
        pltpu.with_memory_space_constraint(gate_up_w, pltpu.HBM),
        pltpu.with_memory_space_constraint(down_w, pltpu.HBM),
    )


def shards(tokens, norm_gain, gate_up, down, routes, route_weights):
    micro_count, token_count, width = tokens.shape
    chosen = routes.shape[-1]
    experts_n = lax.axis_size("expert")
    sections = lax.axis_size("section")
    section_index = lax.axis_index("section")
    chunk_count = micro_count // CHUNK
    rows_n = CHUNK * token_count
    per_expert = CHUNK * CAP
    slots = experts_n * per_expert
    gate_up_w = gate_up[0, 0]
    down_w = down[0, 0]

    pairs = lax.optimization_barrier(routes[0].reshape(micro_count, token_count * chosen))
    order = jnp.arange(token_count * chosen, dtype=jnp.int32)
    same = (pairs[:, :, None] == pairs[:, None, :]) & (order[None, :] < order[:, None])[None]
    rank = jnp.sum(same.astype(jnp.int32), axis=-1)
    block = (jnp.arange(micro_count, dtype=jnp.int32) % CHUNK)[:, None]
    target = (pairs * per_expert + block * CAP + rank).reshape(chunk_count, rows_n, chosen)
    fixed_point = route_weights[0].astype(jnp.float32)
    shares = fixed_point / jnp.sum(fixed_point, axis=-1, keepdims=True)
    shares = shares.reshape(chunk_count, rows_n, chosen)
    chunks = tokens.reshape(chunk_count, rows_n, width)

    slot_ids = jnp.arange(slots, dtype=jnp.int32)

    section_scalar = section_index.reshape(1).astype(jnp.int32)

    def step(tick_number, incoming, fresh_input, results, ahead):
        chunk_here = tick_number - section_index
        clamped = jnp.clip(chunk_here, 0, chunk_count - 1)
        target_rows = lax.dynamic_index_in_dim(target, clamped, 0, keepdims=False)
        share_rows = lax.dynamic_index_in_dim(shares, clamped, 0, keepdims=False)
        mixing = sum(
            jnp.where(slot_ids[None, :] == target_rows[:, k : k + 1], share_rows[:, k : k + 1], 0.0)
            for k in range(chosen)
        )
        mixing = jnp.concatenate(split_three(mixing), axis=0)
        outgoing, stream = place(
            section_scalar, incoming, fresh_input, norm_gain, target_rows.T, experts_n
        )
        active = jnp.logical_and(chunk_here >= 0, chunk_here < chunk_count)
        kept = lax.dynamic_index_in_dim(results, clamped, 0, keepdims=False)
        place_at = clamped.astype(jnp.uint32)
        if ahead:
            outgoing, mixing, kept, active, place_at = lax.optimization_barrier(
                (outgoing, mixing, kept, active, place_at)
            )
        arrived = lax.all_to_all(outgoing, "expert", split_axis=0, concat_axis=0, tiled=True)
        computed = expert_ffn(arrived, gate_up_w, down_w)
        returned = lax.all_to_all(computed, "expert", split_axis=0, concat_axis=0, tiled=True)
        output_rows = combine(returned, mixing, stream)
        results = lax.dynamic_update_slice(
            results,
            jnp.where(active, output_rows, kept)[None],
            (place_at, jnp.uint32(0), jnp.uint32(0)),
        )
        return output_rows, results

    def relayed(tick_number, carried):
        previous, results = carried
        incoming = lax.ppermute(
            previous, "section", [(s, (s + 1) % sections) for s in range(sections)]
        )
        fresh_input = lax.dynamic_index_in_dim(
            chunks, jnp.minimum(tick_number, chunk_count - 1), 0, keepdims=False
        )
        return step(tick_number, incoming, fresh_input, results, True)

    results = jnp.zeros((chunk_count, rows_n, width), jnp.bfloat16)
    carried = step(0, jnp.zeros_like(chunks[0]), chunks[0], results, False)
    carried = lax.fori_loop(1, chunk_count + sections - 1, relayed, carried)
    return carried[1].reshape(1, micro_count, token_count, width)


def solution(mesh):
    return jax.shard_map(
        shards,
        mesh=mesh,
        in_specs=(
            P(None, "expert", None),
            P("section", None),
            P("section", "expert", None, None),
            P("section", "expert", None, None),
            P("section", None, "expert", None),
            P("section", None, "expert", None),
        ),
        out_specs=P("section", None, "expert", None),
        check_vma=False,
    )
```
